32 devices in a mesh: row: 8 (over y, x, core), col: 4 (over z).
Axes of the slice: x: 2, y: 2, z: 4, core: 2. Of those that a mesh axis runs over, the one named last changes fastest.
Arguments:
- legendre: bfloat16 [4, 128, 89, 8, 128], P(None, 'col', None, 'row'), may hold values from -6 to 6
- longitude: float32 [512], replicated, may hold values from -3.140625 to 3.140625
- obs_weight: float32 [512], replicated, may hold values from 0.1 to 1.9
- span_weight: float32 [8], replicated, may hold values from 0.3 to 3
- span_of: int32 [512], replicated, may hold values from 0 to 7
- tile_order: int32 [712], replicated, may hold values from 0 to 711, each once
- slab_start: int32 [1], replicated, may hold values from 0 to 704
- resident: float32 [89, 8, 4, 128, 128], P(None, 'row', 'col'), may hold values from -6 to 6
Outputs:
- updated: float32 [89, 8, 4, 128, 128], P(None, 'row', 'col')
The draws below stay inside these ranges and needn't reach their ends.
Inputs may be any that keep to these rules, and one draw needn't show every extreme that they name: tile_order is a permutation of the slot positions.
All inputs are finite; a program needn't handle non-finite values.
Results may differ from the reference program's by a relative error of at most 0.00074.
Values may be sent and summed in bfloat16 or wider, within the bound.
No kernel may reach another device: no remote copies, remote signals or barrier semaphores. Data moves between devices by JAX's collectives and lax.ppermute only.
A program may use at most 64 MiB of HBM per device.

```python
import math
import jax
import jax.numpy as jnp
from jax import lax

DEGREE = 300
UNK = 90600
TILE = 128
SPAN = 128
BLOCKS = 4
GROUPS = 8
OBS = 512
TILES = 708
ROW_SLOTS = 89
TILES_PAD = 712
N_ROW = 8
N_COL = 4


def with_ends(values, own_key, low, high):
    spot = [jax.random.randint(jax.random.fold_in(own_key, axis), (), 0, length) for axis, length in enumerate(values.shape)]
    widest = values.shape.index(max(values.shape))
    neighbour = spot[:widest] + [(spot[widest] + 1) % values.shape[widest]] + spot[widest + 1:]
    return values.at[tuple(spot)].set(low).at[tuple(neighbour)].set(high)


def block_scale(stream_key, dims, cuts, least, largest):
    def one(position, shards_of):
        draws = jax.random.uniform(jax.random.fold_in(jax.random.fold_in(stream_key, 6), position), (shards_of,), jnp.float32, least / len(cuts), largest / len(cuts))
        return jnp.repeat(jnp.exp(draws), dims[position] // shards_of).reshape((-1,) + (1,) * (len(dims) - position - 1))

    factor_of = one(*cuts[0])
    for cut in cuts[1:]:
        factor_of = factor_of * one(*cut)
    return factor_of


def gaussian(own_key, dims, scale, bound, split=(), kind=jnp.bfloat16):
    entries = jax.random.normal(own_key, dims, jnp.float32) * scale
    if len(split) > 0:
        entries = block_scale(own_key, dims, split, -0.22, 0.18) * entries
    return jnp.clip(entries, min=-bound, max=bound).astype(kind)


def setup_inputs(seed: int = 0) -> dict:
    key_list = jax.random.split(jax.random.key(seed), 9)
    return {
        "legendre": gaussian(key_list[0], (BLOCKS, SPAN, ROW_SLOTS, N_ROW, TILE), 1.0, 6.0, ((1, 4), (3, 8))),
        "longitude": jnp.clip(jax.random.uniform(key_list[1], (OBS,), jnp.float32, -3.140625, 3.140625), -3.140625, 3.140625),
        "obs_weight": jnp.clip(1.0 + 0.18 * jax.random.normal(key_list[2], (OBS,), jnp.float32), 0.1, 1.9),
        "span_weight": jnp.clip(jnp.exp(jax.random.uniform(key_list[3], (GROUPS,), jnp.float32, math.log(0.3), math.log(3.0))), 0.3, 3.0),
        "span_of": with_ends(jax.random.randint(key_list[4], (OBS,), 0, GROUPS), jax.random.fold_in(key_list[4], 1), 0, GROUPS - 1).astype(jnp.int32),
        "tile_order": jax.random.permutation(key_list[5], TILES_PAD).astype(jnp.int32),
        "slab_start": jax.random.randint(key_list[6], (1,), 0, TILES - N_COL + 1).astype(jnp.int32),
        "resident": gaussian(key_list[7], (ROW_SLOTS, N_ROW, N_COL, TILE, TILE), 1.0, 6.0, ((1, 8), (2, 4)), jnp.float32),
    }


def reference(legendre, longitude, obs_weight, span_weight, span_of, tile_order, slab_start, resident):
    slot_total = ROW_SLOTS * N_ROW
    unknown = tile_order[:, None] * TILE + jnp.arange(TILE, dtype=jnp.int32)[None, :]
    orders = (unknown % (DEGREE + 1)).astype(jnp.float32).reshape(1, slot_total * TILE)
    is_valid = (unknown < UNK).reshape(1, slot_total * TILE)
    values = legendre.reshape(OBS, slot_total * TILE).astype(jnp.float32)
    design = jnp.where(is_valid, values * jnp.cos(longitude[:, None] * orders), 0.0).astype(jnp.bfloat16)
    matches = span_of[:, None] == jnp.arange(GROUPS, dtype=jnp.int32)[None, :]
    factor = lax.optimization_barrier(jnp.sum(jnp.where(matches, span_weight[None, :], 0.0), axis=1))
    weight = obs_weight * factor * (0.25 / math.sqrt(OBS))
    targets = slab_start[0] + jnp.arange(N_COL, dtype=jnp.int32)
    places = jnp.arange(slot_total, dtype=jnp.int32)
    positions = lax.optimization_barrier(jnp.sum(jnp.where(tile_order[None, :] == targets[:, None], places[None, :], 0), axis=1)).astype(jnp.int32)
    columns = design.reshape(OBS, slot_total, TILE)[:, positions, :]
    weighted = (weight[:, None, None] * columns.astype(jnp.float32)).astype(jnp.bfloat16)
    products = lax.dot_general(design.astype(jnp.float32), weighted.reshape(OBS, N_COL * TILE).astype(jnp.float32), (((0,), (0,)), ((), ())), precision=lax.Precision.HIGHEST, preferred_element_type=jnp.float32)
    products = products.reshape(ROW_SLOTS, N_ROW, TILE, N_COL, TILE).transpose(0, 1, 3, 2, 4)
    in_lower = tile_order.reshape(ROW_SLOTS, N_ROW)[:, :, None] >= targets[None, None, :]
    return resident + jnp.where(in_lower[:, :, :, None, None], products, 0.0)
```

```python
import functools
import math

import jax
import jax.numpy as jnp
from jax import lax
from jax.experimental import pallas as pl
from jax.experimental.pallas import tpu as pltpu
from jax.sharding import PartitionSpec as P


DEGREE = 300
UNK = 90600
PERIOD = DEGREE + 1


def whole(space=pltpu.VMEM):
    return pl.BlockSpec(memory_space=space)


def lookup_weights(obs_weight, span_weight, span_of):
    group_count = span_weight.shape[0]
    matches = span_of[:, None] == jnp.arange(group_count, dtype=jnp.int32)[None, :]
    factor = jnp.sum(jnp.where(matches, span_weight[None, :], 0.0), axis=1)
    return obs_weight * factor * (0.25 / math.sqrt(obs_weight.shape[0]))


def first_counts(slot_count):
    return max(2, (slot_count * 16) // 100), max(2, (slot_count * 9) // 100)


def rest_counts(slot_count):
    most = slot_count - first_counts(slot_count)[0]
    counts = [count for count in (0,) + tuple(range(8, most, 11)) if count <= most - 6]
    return counts + [most]


def chunk_sizes(total, second):
    if total <= second + 1:
        return [total] if total else []
    if total <= second + 12:
        return [second, total - second]
    left = total - second - 6
    count = -(-left // 22)
    return [second] + [left * (k + 1) // count - left * k // count for k in range(count)] + [6]


def design_tile(tile, slot, legendre, table):
    blocks, _, rows, lanes = legendre.shape
    start = lax.rem(tile * lanes, PERIOD)
    base = start // lanes
    shift = start - base * lanes
    turn = lax.rem(lanes - shift, lanes)
    lane = lax.broadcasted_iota(jnp.int32, (blocks * rows, lanes), 1)
    low = pltpu.roll(table[base], turn, 1)
    high = pltpu.roll(table[base + 1], turn, 1)
    wave = jnp.where(lane < lanes - shift, low, high)
    values = legendre[:, slot].astype(jnp.float32).reshape(blocks * rows, lanes)
    result = jnp.where(lane < UNK - tile * lanes, values * wave, 0.0)
    return result.astype(jnp.bfloat16)


def plan_kernel(
    counts, first, row_count, slab_start, order, legendre, table, weight,
    listed, info, output,
):
    lanes = legendre.shape[3]
    total = order.shape[0]
    width = listed.shape[1]
    start = slab_start[0]
    row = lax.axis_index("row")
    col = lax.axis_index("col")
    tiles = order[...].reshape(1, total)
    spot = lax.broadcasted_iota(jnp.int32, (1, total), 1)
    needed = (tiles >= start) & (tiles * lanes < UNK)
    rows = lax.broadcasted_iota(jnp.int32, (row_count, total), 0)
    matches = jnp.broadcast_to(jnp.where(needed, 1, 0), rows.shape)
    matches = jnp.where(lax.rem(spot, row_count) == rows, matches, 0)
    most = jnp.max(jnp.sum(matches, axis=1))
    choice = jnp.int32(0)
    for below in counts[:-1]:
        choice += jnp.where(most > first + below, 1, 0)

    mine = lax.rem(spot, row_count) == row
    own = jnp.where(needed & mine, 1.0, 0.0)
    before = jnp.dot(
        jnp.broadcast_to(own, (8, total)).astype(jnp.bfloat16),
        (
            lax.broadcasted_iota(jnp.int32, (total, total), 0)
            < lax.broadcasted_iota(jnp.int32, (total, total), 1)
        ).astype(jnp.float32).astype(jnp.bfloat16),
        preferred_element_type=jnp.float32,
    )[:1]
    slot = (spot // row_count).astype(jnp.float32)
    target = jnp.where(needed, before, jnp.sum(own) + slot - before)
    target = jnp.where(mine, target, -1.0)
    ids = lax.broadcasted_iota(jnp.int32, (width, total), 0).astype(jnp.float32)
    hits = jnp.where(ids == target, 1.0, 0.0)
    pair = lax.broadcasted_iota(jnp.int32, (8, total), 0)
    pair = jnp.where(pair == 0, slot, tiles.astype(jnp.float32))
    found = lax.dot_general(
        pair, hits, (((1,), (1,)), ((), ())),
        precision=lax.Precision.HIGHEST, preferred_element_type=jnp.float32,
    )
    listed[...] = found.astype(jnp.int32)
    info[...] = jnp.broadcast_to(choice, info.shape)

    col_count = output.shape[0]
    half = col_count // 2
    is_right = col >= half
    for place in range(col_count):
        near_left = place if place < half else col_count - 1 - (place - half)
        near_right = col_count - 1 - near_left
        tile = start + jnp.where(is_right, near_right, near_left)
        position = jnp.sum(jnp.where(tiles == tile, spot, 0))
        column = design_tile(tile, position // row_count, legendre, table)
        column = weight[...] * column.astype(jnp.float32)
        column = jnp.where(lax.rem(position, row_count) == row, column, 0.0)
        output[place] = column.astype(jnp.bfloat16)


def design_kernel(offset, listed, legendre, table, output):
    def step(index, carry):
        output[index] = design_tile(
            listed[1, offset + index], listed[0, offset + index], legendre, table
        )
        return carry

    lax.fori_loop(0, output.shape[0], step, 0)


def factor_kernel(inner, half, *refs):
    streams, output = refs[:-1], refs[-1]
    rows, lanes = streams[0].shape[1:]
    col = lax.axis_index("col")
    spot = jnp.where(col >= half, 2 * half - 1 - col, col)
    for index, stream in enumerate(streams):
        here = pl.ds(index * rows, rows)
        output[here, :lanes] = stream[spot]
        if 1 <= index <= inner:
            output[here, lanes:] = jnp.zeros_like(stream[0])
        else:
            output[here, lanes:] = stream[0]


def stacked(streams, first, width):
    return jnp.concatenate(
        [jnp.concatenate([s[first + k] for s in streams], 0) for k in range(width)], 1
    )


def product_kernel(factor, *refs):
    streams, own, end = refs[:-2], refs[-2], refs[-1]
    lanes = own.shape[1]
    size = own.shape[0]

    def piece(first, width):
        both = lax.dot_general(
            stacked(streams, first, width), factor[...],
            (((0,), (0,)), ((), ())), preferred_element_type=jnp.float32,
        )
        for k in range(width):
            own[first + k] = both[k * lanes : (k + 1) * lanes, :lanes]
            end[first + k] = both[k * lanes : (k + 1) * lanes, lanes:]

    def step(index, carry):
        piece(2 * index, 2)
        return carry

    lax.fori_loop(0, size // 2, step, 0)
    if size % 2:
        piece(size - 1, 1)


def copy_kernel(offset, listed, resident, output, held, ins, outs):
    size = held.shape[0]

    def fetch(index):
        slot = listed[0, offset + index]
        return pltpu.make_async_copy(resident.at[slot], held.at[index], ins.at[index])

    def store(index):
        slot = listed[0, offset + index]
        return pltpu.make_async_copy(held.at[index], output.at[slot], outs.at[index])

    @pl.loop(0, size)
    def _(index):
        fetch(index).start()

    @pl.loop(0, size)
    def _(index):
        fetch(index).wait()
        store(index).start()

    @pl.loop(0, size)
    def _(index):
        store(index).wait()


def update_kernel(
    offset, listed, slab_start, own, extra, resident, *refs,
):
    output, own_held, extra_held, old, new, ins, outs, more = refs[-8:]
    size = old.shape[0]
    lanes = old.shape[1]
    column = slab_start[0] + lax.axis_index("col")
    own_copy = pltpu.make_async_copy(own, own_held, more.at[0])
    extra_copy = pltpu.make_async_copy(extra, extra_held, more.at[1])

    def fetch(index):
        return pltpu.make_async_copy(
            resident.at[listed[0, offset + index]], old.at[index], ins.at[index]
        )

    def store(index):
        return pltpu.make_async_copy(
            new.at[index], output.at[listed[0, offset + index]], outs.at[index]
        )

    own_copy.start()
    extra_copy.start()

    @pl.loop(0, size)
    def _(index):
        fetch(index).start()

    own_copy.wait()
    extra_copy.wait()

    @pl.loop(0, size)
    def _(index):
        fetch(index).wait()
        tile = listed[1, offset + index]
        keep = (tile >= column) & (tile * lanes < UNK)
        change = own_held[index] + extra_held[index]
        new[index] = old[index] + jnp.where(keep, change, 0.0)
        store(index).start()

    @pl.loop(0, size)
    def _(index):
        store(index).wait()


def per_device(
    legendre, longitude, obs_weight, span_weight, span_of, tile_order, slab_start, resident
):
    block_count, shard_rows, slot_count, _, lanes = legendre.shape
    row_count = lax.axis_size("row")
    col_count = lax.axis_size("col")
    col_index = lax.axis_index("col")
    half = col_count // 2
    block_rows = shard_rows * col_count
    own_rows = block_count * shard_rows
    inner = half - 1
    bf16 = jnp.bfloat16
    smem, vmem, anywhere = whole(pltpu.SMEM), whole(), whole(pl.ANY)

    def mirrored(pairs):
        other = [(col_count - 1 - a, col_count - 1 - b) for a, b in pairs]
        return pairs + other

    inward = mirrored([(i, i + 1) for i in range(half - 1)])
    middles = [mirrored([(half - 1 - t, half)]) for t in range(half)]
    outward = mirrored([(i, i - 1) for i in range(2, half)])
    last_hop = mirrored([(1, 0)])

    def shift(value, pairs, axis="col"):
        return lax.ppermute(value, axis, pairs)

    def streams_of(whole_item, near, far):
        ins = []
        for _ in range(inner):
            ins.append(shift(ins[-1] if ins else whole_item, inward))
        mids = [shift(far(whole_item), pairs) for pairs in middles]
        froms = []
        for t in range(col_count - 2):
            piece = mids[t] if t < half else None
            if outward:
                moved = near(whole_item) if t == 0 else froms[-1]
                moved = shift(moved, outward)
                piece = moved if piece is None else piece + moved
            froms.append(piece)
        return [near(item) for item in [whole_item] + ins], froms

    def same(item):
        return item

    def own_part(values):
        values = values.reshape(block_count, block_rows)
        return lax.dynamic_slice_in_dim(values, col_index * shard_rows, shard_rows, 1)

    weights = own_part(lookup_weights(obs_weight, span_weight, span_of))
    weights = jnp.broadcast_to(weights.reshape(own_rows, 1), (own_rows, lanes))
    pages = PERIOD // lanes + 2
    lane_orders = jnp.arange(pages * lanes, dtype=jnp.int32) % PERIOD
    lane_orders = lane_orders.astype(jnp.float32).reshape(pages, 1, lanes)
    table = jnp.cos(own_part(longitude).reshape(1, own_rows, 1) * lane_orders)

    values = legendre.transpose(0, 2, 3, 1, 4).reshape(block_count, slot_count, shard_rows, lanes)
    old = resident.reshape(slot_count, lanes, lanes)
    first, second = first_counts(slot_count)
    counts = rest_counts(slot_count)
    tile_shape = (own_rows, lanes)

    def tiles_of(size):
        return jax.ShapeDtypeStruct((size,) + tile_shape, bf16)

    def held(size):
        return pltpu.VMEM((size, lanes, lanes), jnp.float32)

    def sems(size):
        return pltpu.SemaphoreType.DMA((size,))

    def design(offset, size, listed, values, table):
        return pl.pallas_call(
            functools.partial(design_kernel, offset),
            out_shape=tiles_of(size),
            in_specs=[smem] + [vmem] * 2,
            out_specs=vmem,
            name="design",
        )(listed, values, table)

    listed, info, both = pl.pallas_call(
        functools.partial(plan_kernel, counts, first, row_count),
        out_shape=[
            jax.ShapeDtypeStruct((8, -(-slot_count // 128) * 128), jnp.int32),
            jax.ShapeDtypeStruct((1, 128), jnp.int32),
            tiles_of(col_count),
        ],
        in_specs=[smem] + [vmem] * 4,
        out_specs=[vmem] * 3,
        name="plan",
    )(slab_start, tile_order, values, table, weights)

    own_first = design(0, first, listed, values, table)
    nears, froms = streams_of(own_first, same, same)
    streams_first = nears + froms
    bit = 1
    while bit < row_count:
        pairs = [(r, r ^ bit) for r in range(row_count)]
        both = both + shift(both, pairs, "row")
        bit *= 2
    nears, froms = streams_of(both, lambda x: x[:half], lambda x: x[half:])
    factors = nears + froms
    factor = pl.pallas_call(
        functools.partial(factor_kernel, inner, half),
        out_shape=jax.ShapeDtypeStruct((len(factors) * own_rows, 2 * lanes), bf16),
        in_specs=[vmem] * len(factors),
        out_specs=vmem,
        name="factor",
    )(*factors)

    def copy_rest(offset, listed, old):
        size = slot_count - offset
        if not size:
            return []
        output = pl.pallas_call(
            functools.partial(copy_kernel, offset),
            in_specs=[smem, anywhere],
            out_specs=anywhere,
            out_shape=jax.ShapeDtypeStruct(old.shape, old.dtype),
            scratch_shapes=[held(size), sems(size), sems(size)],
        )(listed, old)
        return [output]

    def multiply(factor, streams):
        product = jax.ShapeDtypeStruct((streams[0].shape[0], lanes, lanes), jnp.float32)
        return pl.pallas_call(
            product_kernel,
            out_shape=[product, product],
            in_specs=[vmem] * (1 + len(streams)),
            out_specs=[vmem] * 2,
            name="product",
        )(factor, *streams)

    def update(offset, listed, slab_start, own, extra, old, previous):
        size = own.shape[0]
        return pl.pallas_call(
            functools.partial(update_kernel, offset),
            in_specs=[smem] * 2 + [anywhere] * (3 + len(previous)),
            out_specs=anywhere,
            out_shape=jax.ShapeDtypeStruct(old.shape, old.dtype),
            scratch_shapes=[held(size)] * 4 + [sems(size), sems(size), sems(2)],
            input_output_aliases={5: 0} if previous else {},
            name="update",
        )(listed, slab_start, own, extra, old, *previous)

    def branch(total):
        def run(factor, streams_first, listed, slab_start, old, values, table):
            output = copy_rest(first + total, listed, old)
            waiting, offset = [], 0
            for k, size in enumerate([first] + chunk_sizes(total, second)):
                streams = streams_first
                if k > 0:
                    piece = design(offset, size, listed, values, table)
                    nears, froms = streams_of(piece, same, same)
                    streams = nears + froms
                own, end = multiply(factor, streams)
                waiting.append((k, offset, own, shift(end, last_hop)))
                offset += size
            for k, offset, own, extra in waiting:
                output = [update(offset, listed, slab_start, own, extra, old, output)]
            return output[0]

        return run

    output = lax.switch(
        info[0, 0],
        [branch(total) for total in counts],
        factor, streams_first, listed, slab_start, old, values, table,
    )
    return output.reshape(resident.shape)


def solution(mesh):
    placed = (
        P(None, "col", None, "row", None),
        P(),
        P(),
        P(),
        P(),
        P(),
        P(),
        P(None, "row", "col", None, None),
    )
    return jax.shard_map(
        per_device,
        mesh=mesh,
        in_specs=placed,
        out_specs=P(None, "row", "col", None, None),
        check_vma=False,
    )
```

```python
import functools
import math

import jax
import jax.numpy as jnp
from jax import lax
from jax.experimental import pallas as pl
from jax.experimental.pallas import tpu as pltpu
from jax.sharding import PartitionSpec as P


DEGREE = 300
UNK = 90600
PERIOD = DEGREE + 1


def whole(space=pltpu.VMEM):
    return pl.BlockSpec(memory_space=space)


def lookup_weights(obs_weight, span_weight, span_of):
    group_count = span_weight.shape[0]
    matches = span_of[:, None] == jnp.arange(group_count, dtype=jnp.int32)[None, :]
    factor = jnp.sum(jnp.where(matches, span_weight[None, :], 0.0), axis=1)
    return obs_weight * factor * (0.25 / math.sqrt(obs_weight.shape[0]))


def first_counts(slot_count):
    return max(2, (slot_count * 12) // 100), max(2, (slot_count * 14) // 100)


def totals_of(slot_count):
    first, second = first_counts(slot_count)
    counts = [first] + list(range(first + second, slot_count - 5, 11))
    return counts + [slot_count]


def chunk_sizes(total, first, second):
    sizes = [first, second][: 1 if total <= first else 2]
    left = total - sum(sizes)
    if left <= 12:
        return sizes + [left] * (left > 0)
    left -= 6
    count = -(-left // 21)
    return sizes + [left * (k + 1) // count - left * k // count for k in range(count)] + [6]


def design_tile(tile, slot, legendre, table):
    blocks, _, rows, lanes = legendre.shape
    start = lax.rem(tile * lanes, PERIOD)
    base = start // lanes
    shift = start - base * lanes
    turn = lax.rem(lanes - shift, lanes)
    lane = lax.broadcasted_iota(jnp.int32, (blocks * rows, lanes), 1)
    low = pltpu.roll(table[base], turn, 1)
    high = pltpu.roll(table[base + 1], turn, 1)
    wave = jnp.where(lane < lanes - shift, low, high)
    values = legendre[:, slot].astype(jnp.float32).reshape(blocks * rows, lanes)
    result = jnp.where(lane < UNK - tile * lanes, values * wave, 0.0)
    return result.astype(jnp.bfloat16)


def plan_kernel(
    counts, row_count, slab_start, order, legendre, table, weight,
    listed, info, output,
):
    lanes = legendre.shape[3]
    total = order.shape[0]
    width = listed.shape[1]
    start = slab_start[0]
    row = lax.axis_index("row")
    col = lax.axis_index("col")
    tiles = order[...].reshape(1, total)
    spot = lax.broadcasted_iota(jnp.int32, (1, total), 1)
    needed = (tiles >= start) & (tiles * lanes < UNK)
    rows = lax.broadcasted_iota(jnp.int32, (row_count, total), 0)
    matches = jnp.broadcast_to(jnp.where(needed, 1, 0), rows.shape)
    matches = jnp.where(lax.rem(spot, row_count) == rows, matches, 0)
    most = jnp.max(jnp.sum(matches, axis=1))
    choice = jnp.int32(0)
    for below in counts[:-1]:
        choice += jnp.where(most > below, 1, 0)

    mine = lax.rem(spot, row_count) == row
    own = jnp.where(needed & mine, 1.0, 0.0)
    before = jnp.dot(
        jnp.broadcast_to(own, (8, total)).astype(jnp.bfloat16),
        (
            lax.broadcasted_iota(jnp.int32, (total, total), 0)
            < lax.broadcasted_iota(jnp.int32, (total, total), 1)
        ).astype(jnp.float32).astype(jnp.bfloat16),
        preferred_element_type=jnp.float32,
    )[:1]
    slot = (spot // row_count).astype(jnp.float32)
    target = jnp.where(needed, before, jnp.sum(own) + slot - before)
    target = jnp.where(mine, target, -1.0)
    ids = lax.broadcasted_iota(jnp.int32, (width, total), 0).astype(jnp.float32)
    hits = jnp.where(ids == target, 1.0, 0.0)
    pair = lax.broadcasted_iota(jnp.int32, (8, total), 0)
    pair = jnp.where(pair == 0, slot, tiles.astype(jnp.float32))
    found = lax.dot_general(
        pair, hits, (((1,), (1,)), ((), ())),
        precision=lax.Precision.HIGHEST, preferred_element_type=jnp.float32,
    )
    listed[...] = found.astype(jnp.int32)
    info[...] = jnp.broadcast_to(choice, info.shape)

    col_count = output.shape[0]
    half = col_count // 2
    is_right = col >= half
    for place in range(col_count):
        near_left = place if place < half else col_count - 1 - (place - half)
        near_right = col_count - 1 - near_left
        tile = start + jnp.where(is_right, near_right, near_left)
        position = jnp.sum(jnp.where(tiles == tile, spot, 0))
        column = design_tile(tile, position // row_count, legendre, table)
        column = weight[...] * column.astype(jnp.float32)
        column = jnp.where(lax.rem(position, row_count) == row, column, 0.0)
        output[place] = column.astype(jnp.bfloat16)


def design_kernel(offset, listed, legendre, table, output):
    def step(index, carry):
        output[index] = design_tile(
            listed[1, offset + index], listed[0, offset + index], legendre, table
        )
        return carry

    lax.fori_loop(0, output.shape[0], step, 0)


def factor_kernel(inner, half, *refs):
    streams, output = refs[:-1], refs[-1]
    rows, lanes = streams[0].shape[1:]
    col = lax.axis_index("col")
    spot = jnp.where(col >= half, 2 * half - 1 - col, col)
    for index, stream in enumerate(streams):
        here = pl.ds(index * rows, rows)
        kept = (spot > 0) | (index == 0)
        output[here, :lanes] = jnp.where(kept, stream[spot], jnp.zeros_like(stream[0]))
        if 1 <= index <= inner:
            output[here, lanes:] = jnp.zeros_like(stream[0])
        else:
            output[here, lanes:] = stream[0]


def stacked(streams, first, width):
    return jnp.concatenate(
        [jnp.concatenate([s[first + k] for s in streams], 0) for k in range(width)], 1
    )


def product_kernel(factor, *refs):
    streams, own, end = refs[:-2], refs[-2], refs[-1]
    lanes = own.shape[1]
    size = own.shape[0]

    def piece(first, width):
        both = lax.dot_general(
            stacked(streams, first, width), factor[...],
            (((0,), (0,)), ((), ())), preferred_element_type=jnp.float32,
        )
        for k in range(width):
            own[first + k] = both[k * lanes : (k + 1) * lanes, :lanes]
            end[first + k] = both[k * lanes : (k + 1) * lanes, lanes:]

    def step(index, carry):
        piece(2 * index, 2)
        return carry

    lax.fori_loop(0, size // 2, step, 0)
    if size % 2:
        piece(size - 1, 1)


def copy_kernel(offset, listed, resident, output, held, ins, outs):
    size = held.shape[0]

    def fetch(index):
        slot = listed[0, offset + index]
        return pltpu.make_async_copy(resident.at[slot], held.at[index], ins.at[index])

    def store(index):
        slot = listed[0, offset + index]
        return pltpu.make_async_copy(held.at[index], output.at[slot], outs.at[index])

    @pl.loop(0, size)
    def _(index):
        fetch(index).start()

    @pl.loop(0, size)
    def _(index):
        fetch(index).wait()
        store(index).start()

    @pl.loop(0, size)
    def _(index):
        store(index).wait()


def update_kernel(
    offset, listed, slab_start, own, extra, resident, *refs,
):
    output, own_held, extra_held, old, new, ins, outs, more = refs[-8:]
    size = old.shape[0]
    lanes = old.shape[1]
    column = slab_start[0] + lax.axis_index("col")
    own_copy = pltpu.make_async_copy(own, own_held, more.at[0])
    extra_copy = pltpu.make_async_copy(extra, extra_held, more.at[1])

    def fetch(index):
        return pltpu.make_async_copy(
            resident.at[listed[0, offset + index]], old.at[index], ins.at[index]
        )

    def store(index):
        return pltpu.make_async_copy(
            new.at[index], output.at[listed[0, offset + index]], outs.at[index]
        )

    own_copy.start()
    extra_copy.start()

    @pl.loop(0, size)
    def _(index):
        fetch(index).start()

    own_copy.wait()
    extra_copy.wait()

    @pl.loop(0, size)
    def _(index):
        fetch(index).wait()
        tile = listed[1, offset + index]
        keep = (tile >= column) & (tile * lanes < UNK)
        change = own_held[index] + extra_held[index]
        new[index] = old[index] + jnp.where(keep, change, 0.0)
        store(index).start()

    @pl.loop(0, size)
    def _(index):
        store(index).wait()


def per_device(
    legendre, longitude, obs_weight, span_weight, span_of, tile_order, slab_start, resident
):
    block_count, shard_rows, slot_count, _, lanes = legendre.shape
    row_count = lax.axis_size("row")
    col_count = lax.axis_size("col")
    col_index = lax.axis_index("col")
    half = col_count // 2
    block_rows = shard_rows * col_count
    own_rows = block_count * shard_rows
    inner = half - 1
    bf16 = jnp.bfloat16
    smem, vmem, anywhere = whole(pltpu.SMEM), whole(), whole(pl.ANY)

    def mirrored(pairs):
        other = [(col_count - 1 - a, col_count - 1 - b) for a, b in pairs]
        return pairs + other

    inward = mirrored([(i, i + 1) for i in range(half - 1)])
    middles = [mirrored([(half - 1 - t, half)]) for t in range(half)]
    outward = mirrored([(i, i - 1) for i in range(2, half)])
    last_hop = mirrored([(1, 0)])
    filler = last_hop if half == 2 else []

    def shift(value, pairs, axis="col"):
        return lax.ppermute(value, axis, pairs)

    def streams_of(whole_item, near, far, idle=False):
        more = filler if idle else []
        ins = []
        for _ in range(inner):
            ins.append(shift(ins[-1] if ins else whole_item, inward + more))
        mids = [shift(far(whole_item), pairs + more * (t > 0)) for t, pairs in enumerate(middles)]
        froms = []
        for t in range(col_count - 2):
            piece = mids[t] if t < half else None
            if outward:
                moved = near(whole_item) if t == 0 else froms[-1]
                moved = shift(moved, outward)
                piece = moved if piece is None else piece + moved
            froms.append(piece)
        return [near(item) for item in [whole_item] + ins], froms

    def same(item):
        return item

    def own_part(values):
        values = values.reshape(block_count, block_rows)
        return lax.dynamic_slice_in_dim(values, col_index * shard_rows, shard_rows, 1)

    weights = own_part(lookup_weights(obs_weight, span_weight, span_of))
    weights = jnp.broadcast_to(weights.reshape(own_rows, 1), (own_rows, lanes))
    pages = PERIOD // lanes + 2
    lane_orders = jnp.arange(pages * lanes, dtype=jnp.int32) % PERIOD
    lane_orders = lane_orders.astype(jnp.float32).reshape(pages, 1, lanes)
    table = jnp.cos(own_part(longitude).reshape(1, own_rows, 1) * lane_orders)

    values = legendre.transpose(0, 2, 3, 1, 4).reshape(block_count, slot_count, shard_rows, lanes)
    old = resident.reshape(slot_count, lanes, lanes)
    first, second = first_counts(slot_count)
    counts = totals_of(slot_count)
    tile_shape = (own_rows, lanes)

    def tiles_of(size):
        return jax.ShapeDtypeStruct((size,) + tile_shape, bf16)

    def held(size):
        return pltpu.VMEM((size, lanes, lanes), jnp.float32)

    def sems(size):
        return pltpu.SemaphoreType.DMA((size,))

    def design(offset, size, listed, values, table):
        return pl.pallas_call(
            functools.partial(design_kernel, offset),
            out_shape=tiles_of(size),
            in_specs=[smem] + [vmem] * 2,
            out_specs=vmem,
            name="design",
        )(listed, values, table)

    listed, info, both = pl.pallas_call(
        functools.partial(plan_kernel, counts, row_count),
        out_shape=[
            jax.ShapeDtypeStruct((8, -(-slot_count // 128) * 128), jnp.int32),
            jax.ShapeDtypeStruct((1, 128), jnp.int32),
            tiles_of(col_count),
        ],
        in_specs=[smem] + [vmem] * 4,
        out_specs=[vmem] * 3,
        name="plan",
    )(slab_start, tile_order, values, table, weights)

    def collect(factors):
        return pl.pallas_call(
            functools.partial(factor_kernel, inner, half),
            out_shape=jax.ShapeDtypeStruct((len(factors) * own_rows, 2 * lanes), bf16),
            in_specs=[vmem] * len(factors),
            out_specs=vmem,
            name="factor",
        )(*factors)

    def copy_rest(offset, listed, old):
        size = slot_count - offset
        if not size:
            return []
        output = pl.pallas_call(
            functools.partial(copy_kernel, offset),
            in_specs=[smem, anywhere],
            out_specs=anywhere,
            out_shape=jax.ShapeDtypeStruct(old.shape, old.dtype),
            scratch_shapes=[held(size), sems(size), sems(size)],
        )(listed, old)
        return [output]

    def multiply(factor, streams):
        product = jax.ShapeDtypeStruct((streams[0].shape[0], lanes, lanes), jnp.float32)
        return pl.pallas_call(
            product_kernel,
            out_shape=[product, product],
            in_specs=[vmem] * (1 + len(streams)),
            out_specs=[vmem] * 2,
            name="product",
        )(factor, *streams)

    def update(offset, listed, slab_start, own, extra, old, previous):
        size = own.shape[0]
        return pl.pallas_call(
            functools.partial(update_kernel, offset),
            in_specs=[smem] * 2 + [anywhere] * (3 + len(previous)),
            out_specs=anywhere,
            out_shape=jax.ShapeDtypeStruct(old.shape, old.dtype),
            scratch_shapes=[held(size)] * 4 + [sems(size), sems(size), sems(2)],
            input_output_aliases={5: 0} if previous else {},
            name="update",
        )(listed, slab_start, own, extra, old, *previous)

    def branch(total):
        def run(both, listed, slab_start, old, values, table):
            bit = 1
            while bit < row_count:
                pairs = [(r, r ^ bit) for r in range(row_count)]
                both = both + shift(both, pairs, "row")
                bit *= 2
            nears, froms = streams_of(both, lambda x: x[:half], lambda x: x[half:], True)
            factor = collect(nears + froms)
            output = copy_rest(total, listed, old)
            waiting, offset = [], 0
            for k, size in enumerate(chunk_sizes(total, first, second)):
                piece = design(offset, size, listed, values, table)
                nears, froms = streams_of(piece, same, same, k == 0)
                streams = nears + froms
                own, end = multiply(factor, streams)
                waiting.append((k, offset, own, shift(end, last_hop)))
                offset += size
            for k, offset, own, extra in waiting:
                output = [update(offset, listed, slab_start, own, extra, old, output)]
            return output[0]

        return run

    output = lax.switch(
        info[0, 0],
        [branch(total) for total in counts],
        both, listed, slab_start, old, values, table,
    )
    return output.reshape(resident.shape)


def solution(mesh):
    placed = (
        P(None, "col", None, "row", None),
        P(),
        P(),
        P(),
        P(),
        P(),
        P(),
        P(None, "row", "col", None, None),
    )
    return jax.shard_map(
        per_device,
        mesh=mesh,
        in_specs=placed,
        out_specs=P(None, "row", "col", None, None),
        check_vma=False,
    )
```

```python
import functools
import math

import jax
import jax.numpy as jnp
from jax import lax
from jax.experimental import pallas as pl
from jax.experimental.pallas import tpu as pltpu
from jax.sharding import PartitionSpec as P


DEGREE = 300
UNK = 90600
PERIOD = DEGREE + 1


def whole(space=pltpu.VMEM):
    return pl.BlockSpec(memory_space=space)


def totals_of(slot_count):
    counts = [9, 19, 29] + list(range(40, slot_count - 4, 12))
    return [count for count in counts if count < slot_count] + [slot_count]


def chunk_sizes(total):
    count = max(1, -(-(total - 2) // 13))
    less = max(1, (total - 4 * (count // 2)) // count)
    sizes = [less + 4 * (k % 2) if count > 1 else total for k in range(count)]
    for k in (list(range(1, count, 2)) + list(range(0, count, 2)))[: total - sum(sizes)]:
        sizes[k] += 1
    return sizes


def design_tile(tile, slot, legendre, table):
    blocks, _, rows, lanes = legendre.shape
    start = lax.rem(tile * lanes, PERIOD)
    base = start // lanes
    shift = start - base * lanes
    turn = lax.rem(lanes - shift, lanes)
    lane = lax.broadcasted_iota(jnp.int32, (blocks * rows, lanes), 1)
    low = pltpu.roll(table[base], turn, 1)
    high = pltpu.roll(table[base + 1], turn, 1)
    wave = jnp.where(lane < lanes - shift, low, high)
    values = legendre[:, slot].astype(jnp.float32).reshape(blocks * rows, lanes)
    result = jnp.where(lane < UNK - tile * lanes, values * wave, 0.0)
    return result.astype(jnp.bfloat16)


def plan_kernel(
    counts, row_count, slab_start, span_weight, order, obs_weight, span_of, legendre, table,
    listed, info, output,
):
    lanes = legendre.shape[3]
    total = order.shape[0]
    width = listed.shape[1]
    start = slab_start[0]
    row = lax.axis_index("row")
    col = lax.axis_index("col")
    tiles = order[...].reshape(1, total)
    spot = lax.broadcasted_iota(jnp.int32, (1, total), 1)
    needed = (tiles >= start) & (tiles * lanes < UNK)
    rows = lax.broadcasted_iota(jnp.int32, (row_count, total), 0)
    matches = jnp.broadcast_to(jnp.where(needed, 1, 0), rows.shape)
    matches = jnp.where(lax.rem(spot, row_count) == rows, matches, 0)
    most = jnp.max(jnp.sum(matches, axis=1))
    choice = jnp.int32(0)
    for below in counts[:-1]:
        choice += jnp.where(most > below, 1, 0)

    mine = lax.rem(spot, row_count) == row
    own = jnp.where(needed & mine, 1.0, 0.0)
    before = jnp.dot(
        jnp.broadcast_to(own, (8, total)).astype(jnp.bfloat16),
        (
            lax.broadcasted_iota(jnp.int32, (total, total), 0)
            < lax.broadcasted_iota(jnp.int32, (total, total), 1)
        ).astype(jnp.float32).astype(jnp.bfloat16),
        preferred_element_type=jnp.float32,
    )[:1]
    slot = (spot // row_count).astype(jnp.float32)
    target = jnp.where(needed, before, jnp.sum(own) + slot - before)
    target = jnp.where(mine, target, -1.0)
    ids = lax.broadcasted_iota(jnp.int32, (width, total), 0).astype(jnp.float32)
    hits = jnp.where(ids == target, 1.0, 0.0)
    pair = lax.broadcasted_iota(jnp.int32, (8, total), 0)
    pair = jnp.where(pair == 0, slot, tiles.astype(jnp.float32))
    found = lax.dot_general(
        pair, hits, (((1,), (1,)), ((), ())),
        precision=lax.Precision.HIGHEST, preferred_element_type=jnp.float32,
    )
    listed[...] = found.astype(jnp.int32)
    info[...] = jnp.broadcast_to(choice, info.shape)

    col_count = output.shape[0]
    half = col_count // 2
    is_right = col >= half
    observations = obs_weight.shape[0]
    blocks, _, shard_rows, _ = legendre.shape
    span = span_of[...].reshape(1, observations)
    factor = jnp.zeros(span.shape, jnp.float32)
    for group in range(span_weight.shape[0]):
        factor += jnp.where(span == group, span_weight[group], 0.0)
    weights = obs_weight[...].reshape(1, observations) * factor
    weights *= 0.25 / math.sqrt(observations)
    shape = (blocks * shard_rows, observations)
    mine = lax.broadcasted_iota(jnp.int32, shape, 0)
    mine = mine // shard_rows * (shard_rows * col_count) + lax.rem(mine, shard_rows)
    mine = mine + col * shard_rows == lax.broadcasted_iota(jnp.int32, shape, 1)
    weight = lax.dot_general(
        jnp.where(mine, 1.0, 0.0), jnp.broadcast_to(weights, (lanes, observations)),
        (((1,), (1,)), ((), ())),
        precision=lax.Precision.HIGHEST, preferred_element_type=jnp.float32,
    )
    for place in range(col_count):
        near_left = place if place < half else col_count - 1 - (place - half)
        near_right = col_count - 1 - near_left
        tile = start + jnp.where(is_right, near_right, near_left)
        position = jnp.sum(jnp.where(tiles == tile, spot, 0))
        column = design_tile(tile, position // row_count, legendre, table)
        column = weight * column.astype(jnp.float32)
        column = jnp.where(lax.rem(position, row_count) == row, column, 0.0)
        output[place] = column.astype(jnp.bfloat16)


def design_kernel(offset, listed, legendre, table, output):
    def step(index, carry):
        output[index] = design_tile(
            listed[1, offset + index], listed[0, offset + index], legendre, table
        )
        return carry

    lax.fori_loop(0, output.shape[0], step, 0)


def factor_kernel(inner, half, *refs):
    streams, output = refs[:-1], refs[-1]
    rows, lanes = streams[0].shape[1:]
    col = lax.axis_index("col")
    spot = jnp.where(col >= half, 2 * half - 1 - col, col)
    for index, stream in enumerate(streams):
        here = pl.ds(index * rows, rows)
        kept = (spot > 0) | (index == 0)
        output[here, :lanes] = jnp.where(kept, stream[spot], jnp.zeros_like(stream[0]))
        if 1 <= index <= inner:
            output[here, lanes:] = jnp.zeros_like(stream[0])
        else:
            output[here, lanes:] = stream[0]


def stacked(streams, first, width):
    return jnp.concatenate(
        [jnp.concatenate([s[first + k] for s in streams], 0) for k in range(width)], 1
    )


def product_kernel(count, factor, *refs):
    streams, following, (own, *ends) = refs[:count], refs[count:-3], refs[-3:]
    lanes = own.shape[1]
    size = own.shape[0]
    col = lax.axis_index("col")
    is_end = (col == 0) | (col == lax.axis_size("col") - 1)

    def piece(first, width):
        both = lax.dot_general(
            stacked(streams, first, width), factor[...],
            (((0,), (0,)), ((), ())), preferred_element_type=jnp.float32,
        )
        for k in range(width):
            own[first + k] = both[k * lanes : (k + 1) * lanes, :lanes]
            end = both[k * lanes : (k + 1) * lanes, lanes:]
            high = end.astype(jnp.bfloat16)
            ends[0][first + k] = high
            ends[1][first + k] = (end - high.astype(jnp.float32)).astype(jnp.bfloat16)

    def step(index, carry):
        piece(2 * index, 2)
        return carry

    lax.fori_loop(0, size // 2, step, 0)
    if size % 2:
        piece(size - 1, 1)
    for later in following:
        @pl.when(is_end)
        def _(later=later):
            ends[0][: later.shape[0]] = later[...]
            ends[1][: later.shape[0]] = later[...]


def copy_kernel(offset, listed, resident, output, held, ins, outs):
    size = held.shape[0]

    def fetch(index):
        slot = listed[0, offset + index]
        return pltpu.make_async_copy(resident.at[slot], held.at[index], ins.at[index])

    def store(index):
        slot = listed[0, offset + index]
        return pltpu.make_async_copy(held.at[index], output.at[slot], outs.at[index])

    @pl.loop(0, size)
    def _(index):
        fetch(index).start()

    @pl.loop(0, size)
    def _(index):
        fetch(index).wait()
        store(index).start()

    @pl.loop(0, size)
    def _(index):
        store(index).wait()


def update_kernel(
    offset, listed, slab_start, own, high, low, resident, *refs,
):
    output, own_held, high_held, low_held, old, new, ins, outs, more = refs[-9:]
    size = old.shape[0]
    lanes = old.shape[1]
    col = lax.axis_index("col")
    column = slab_start[0] + col
    is_end = (col == 0) | (col == lax.axis_size("col") - 1)
    copies = [
        pltpu.make_async_copy(own, own_held, more.at[0]),
        pltpu.make_async_copy(high.at[pl.ds(0, size)], high_held, more.at[1]),
        pltpu.make_async_copy(low.at[pl.ds(0, size)], low_held, more.at[2]),
    ]

    def fetch(index):
        return pltpu.make_async_copy(
            resident.at[listed[0, offset + index]], old.at[index], ins.at[index]
        )

    def store(index):
        return pltpu.make_async_copy(
            new.at[index], output.at[listed[0, offset + index]], outs.at[index]
        )

    for copy in copies:
        copy.start()

    @pl.loop(0, size)
    def _(index):
        fetch(index).start()

    for copy in copies:
        copy.wait()

    @pl.loop(0, size)
    def _(index):
        fetch(index).wait()
        tile = listed[1, offset + index]
        keep = (tile >= column) & (tile * lanes < UNK)
        extra = high_held[index].astype(jnp.float32) + low_held[index].astype(jnp.float32)
        change = own_held[index] + jnp.where(is_end, extra, 0.0)
        new[index] = old[index] + jnp.where(keep, change, 0.0)
        store(index).start()

    @pl.loop(0, size)
    def _(index):
        store(index).wait()


def per_device(
    legendre, longitude, obs_weight, span_weight, span_of, tile_order, slab_start, resident
):
    block_count, shard_rows, slot_count, _, lanes = legendre.shape
    row_count = lax.axis_size("row")
    col_count = lax.axis_size("col")
    col_index = lax.axis_index("col")
    half = col_count // 2
    block_rows = shard_rows * col_count
    own_rows = block_count * shard_rows
    inner = half - 1
    bf16 = jnp.bfloat16
    smem, vmem, anywhere = whole(pltpu.SMEM), whole(), whole(pl.ANY)

    def mirrored(pairs):
        other = [(col_count - 1 - a, col_count - 1 - b) for a, b in pairs]
        return pairs + other

    inward = mirrored([(i, i + 1) for i in range(half - 1)])
    middles = [mirrored([(half - 1 - t, half)]) for t in range(half)]
    outward = mirrored([(i, i - 1) for i in range(2, half)])
    last_hop = mirrored([(1, 0)])
    filler = last_hop if half == 2 else []

    def shift(value, pairs, axis="col"):
        return lax.ppermute(value, axis, pairs)

    def streams_of(whole_item, near, far, idle=False):
        more = filler if idle else []
        ins = []
        for _ in range(inner):
            ins.append(shift(ins[-1] if ins else whole_item, inward + more))
        mids = [shift(far(whole_item), pairs + more * (t > 0)) for t, pairs in enumerate(middles)]
        froms = []
        for t in range(col_count - 2):
            piece = mids[t] if t < half else None
            if outward:
                moved = near(whole_item) if t == 0 else froms[-1]
                moved = shift(moved, outward)
                piece = moved if piece is None else piece + moved
            froms.append(piece)
        return [whole_item] + ins, froms

    def same(item):
        return item

    def own_part(values):
        values = values.reshape(block_count, block_rows)
        return lax.dynamic_slice_in_dim(values, col_index * shard_rows, shard_rows, 1)

    pages = PERIOD // lanes + 2
    lane_orders = jnp.arange(pages * lanes, dtype=jnp.int32) % PERIOD
    lane_orders = lane_orders.astype(jnp.float32).reshape(pages, 1, lanes)
    table = jnp.cos(own_part(longitude).reshape(1, own_rows, 1) * lane_orders)

    values = legendre.transpose(0, 2, 3, 1, 4).reshape(block_count, slot_count, shard_rows, lanes)
    old = resident.reshape(slot_count, lanes, lanes)
    counts = totals_of(slot_count)
    tile_shape = (own_rows, lanes)

    def tiles_of(size):
        return jax.ShapeDtypeStruct((size,) + tile_shape, bf16)

    def held(size):
        return pltpu.VMEM((size, lanes, lanes), jnp.float32)

    def sems(size):
        return pltpu.SemaphoreType.DMA((size,))

    def design(offset, size, listed, values, table):
        return pl.pallas_call(
            functools.partial(design_kernel, offset),
            out_shape=tiles_of(size),
            in_specs=[smem] + [vmem] * 2,
            out_specs=vmem,
            name="design",
        )(listed, values, table)

    listed, info, both = pl.pallas_call(
        functools.partial(plan_kernel, counts, row_count),
        out_shape=[
            jax.ShapeDtypeStruct((8, -(-slot_count // 128) * 128), jnp.int32),
            jax.ShapeDtypeStruct((1, 128), jnp.int32),
            tiles_of(col_count),
        ],
        in_specs=[smem] * 2 + [vmem] * 5,
        out_specs=[vmem] * 3,
        name="plan",
    )(slab_start, span_weight, tile_order, obs_weight, span_of, values, table)

    def collect(factors):
        return pl.pallas_call(
            functools.partial(factor_kernel, inner, half),
            out_shape=jax.ShapeDtypeStruct((len(factors) * own_rows, 2 * lanes), bf16),
            in_specs=[vmem] * len(factors),
            out_specs=vmem,
            name="factor",
        )(*factors)

    def copy_rest(offset, listed, old):
        size = slot_count - offset
        if not size:
            return []
        output = pl.pallas_call(
            functools.partial(copy_kernel, offset),
            in_specs=[smem, anywhere],
            out_specs=anywhere,
            out_shape=jax.ShapeDtypeStruct(old.shape, old.dtype),
            scratch_shapes=[held(size), sems(size), sems(size)],
        )(listed, old)
        return [output]

    def multiply(factor, streams, size, following):
        width = max([size] + [item.shape[0] for item in following])
        return pl.pallas_call(
            functools.partial(product_kernel, len(streams)),
            out_shape=[
                jax.ShapeDtypeStruct((size, lanes, lanes), jnp.float32),
                jax.ShapeDtypeStruct((width, lanes, lanes), bf16),
                jax.ShapeDtypeStruct((width, lanes, lanes), bf16),
            ],
            in_specs=[vmem] * (1 + len(streams) + len(following)),
            out_specs=[vmem] * 3,
            name="product",
        )(factor, *streams, *following)

    def update(offset, listed, slab_start, own, high, low, old, previous):
        size = own.shape[0]
        part = pltpu.VMEM((size, lanes, lanes), bf16)
        return pl.pallas_call(
            functools.partial(update_kernel, offset),
            in_specs=[smem] * 2 + [anywhere] * (4 + len(previous)),
            out_specs=anywhere,
            out_shape=jax.ShapeDtypeStruct(old.shape, old.dtype),
            scratch_shapes=[
                held(size), part, part, held(size), held(size),
                sems(size), sems(size), sems(3),
            ],
            input_output_aliases={6: 0} if previous else {},
            name="update",
        )(listed, slab_start, own, high, low, old, *previous)

    def branch(total):
        sizes = chunk_sizes(total)
        riding = half == 2 and own_rows == lanes

        def run(both, listed, slab_start, old, values, table):
            bit = 1
            while bit < row_count:
                pairs = [(r, r ^ bit) for r in range(row_count)]
                both = both + shift(both, pairs, "row")
                bit *= 2
            nears, froms = streams_of(both, lambda x: x[:half], lambda x: x[half:], True)
            factor = collect(nears + froms)
            offsets = [sum(sizes[:k]) for k in range(len(sizes))]
            designs = [
                design(offset, size, listed, values, table)
                for offset, size in zip(offsets, sizes)
            ]
            done = []
            for k, size in enumerate(sizes):
                if k < 2 or not riding:
                    nears, froms = streams_of(designs[k], same, same, k == 0)
                    streams = nears + froms
                else:
                    passed = shift(designs[k], middles[0])
                    near_end, far_end = done[k - 2][1:]
                    streams = [designs[k], near_end, passed, far_end]
                following = designs[k + 2 : k + 3] if riding else []
                own, high, low = multiply(factor, streams, size, following)
                more = [inward, middles[1]] if riding else [[], []]
                high = shift(high, last_hop + more[0])
                low = shift(low, last_hop + more[1])
                done.append((own, high, low))
            output = copy_rest(total, listed, old)
            for k, (own, high, low) in enumerate(done):
                output = [update(offsets[k], listed, slab_start, own, high, low, old, output)]
            return output[0]

        return run

    output = lax.switch(
        info[0, 0],
        [branch(total) for total in counts],
        both, listed, slab_start, old, values, table,
    )
    return output.reshape(resident.shape)


def solution(mesh):
    placed = (
        P(None, "col", None, "row", None),
        P(),
        P(),
        P(),
        P(),
        P(),
        P(),
        P(None, "row", "col", None, None),
    )
    return jax.shard_map(
        per_device,
        mesh=mesh,
        in_specs=placed,
        out_specs=P(None, "row", "col", None, None),
        check_vma=False,
    )
```

```python
import functools
import math

import jax
import jax.numpy as jnp
from jax import lax
from jax.experimental import pallas as pl
from jax.experimental.pallas import tpu as pltpu
from jax.sharding import PartitionSpec as P


DEGREE = 300
UNK = 90600
PERIOD = DEGREE + 1


def whole(space=pltpu.VMEM):
    return pl.BlockSpec(memory_space=space)


def totals_of(slot_count):
    counts = range(9, slot_count - 6, 16)
    return [count for count in counts if count < slot_count] + [slot_count]


def chunk_sizes(total):
    count = total // 15 + 2 if total > 12 else 1
    less = max(1, (total - 1 * (count // 2)) // count)
    sizes = [less + 1 * (k % 2) if count > 1 else total for k in range(count)]
    for k in (list(range(1, count, 2)) + list(range(0, count, 2)))[: total - sum(sizes)]:
        sizes[k] += 1
    return sizes


def design_tile(tile, slot, legendre, table):
    blocks, _, rows, lanes = legendre.shape
    start = lax.rem(tile * lanes, PERIOD)
    base = start // lanes
    shift = start - base * lanes
    turn = lax.rem(lanes - shift, lanes)
    lane = lax.broadcasted_iota(jnp.int32, (blocks * rows, lanes), 1)
    low = pltpu.roll(table[base], turn, 1)
    high = pltpu.roll(table[base + 1], turn, 1)
    wave = jnp.where(lane < lanes - shift, low, high)
    values = legendre[:, slot].astype(jnp.float32).reshape(blocks * rows, lanes)
    result = jnp.where(lane < UNK - tile * lanes, values * wave, 0.0)
    return result.astype(jnp.bfloat16)


def plan_kernel(
    counts, row_count, slab_start, span_weight, order, obs_weight, span_of, legendre, table,
    listed, info, output,
):
    lanes = legendre.shape[3]
    total = order.shape[0]
    width = listed.shape[1]
    start = slab_start[0]
    row = lax.axis_index("row")
    col = lax.axis_index("col")
    tiles = order[...].reshape(1, total)
    spot = lax.broadcasted_iota(jnp.int32, (1, total), 1)
    needed = (tiles >= start) & (tiles * lanes < UNK)
    rows = lax.broadcasted_iota(jnp.int32, (row_count, total), 0)
    matches = jnp.broadcast_to(jnp.where(needed, 1, 0), rows.shape)
    matches = jnp.where(lax.rem(spot, row_count) == rows, matches, 0)
    most = jnp.max(jnp.sum(matches, axis=1))
    choice = jnp.int32(0)
    for below in counts[:-1]:
        choice += jnp.where(most > below, 1, 0)

    mine = lax.rem(spot, row_count) == row
    own = jnp.where(needed & mine, 1.0, 0.0)
    before = jnp.dot(
        jnp.broadcast_to(own, (8, total)).astype(jnp.bfloat16),
        (
            lax.broadcasted_iota(jnp.int32, (total, total), 0)
            < lax.broadcasted_iota(jnp.int32, (total, total), 1)
        ).astype(jnp.float32).astype(jnp.bfloat16),
        preferred_element_type=jnp.float32,
    )[:1]
    slot = (spot // row_count).astype(jnp.float32)
    target = jnp.where(needed, before, jnp.sum(own) + slot - before)
    target = jnp.where(mine, target, -1.0)
    ids = lax.broadcasted_iota(jnp.int32, (width, total), 0).astype(jnp.float32)
    hits = jnp.where(ids == target, 1.0, 0.0)
    pair = lax.broadcasted_iota(jnp.int32, (8, total), 0)
    pair = jnp.where(pair == 0, slot, tiles.astype(jnp.float32))
    found = lax.dot_general(
        pair, hits, (((1,), (1,)), ((), ())),
        precision=lax.Precision.HIGHEST, preferred_element_type=jnp.float32,
    )
    listed[...] = found.astype(jnp.int32)
    info[...] = jnp.broadcast_to(choice, info.shape)

    col_count = output.shape[0]
    half = col_count // 2
    is_right = col >= half
    observations = obs_weight.shape[0]
    blocks, _, shard_rows, _ = legendre.shape
    span = span_of[...].reshape(1, observations)
    factor = jnp.zeros(span.shape, jnp.float32)
    for group in range(span_weight.shape[0]):
        factor += jnp.where(span == group, span_weight[group], 0.0)
    weights = obs_weight[...].reshape(1, observations) * factor
    weights *= 0.25 / math.sqrt(observations)
    shape = (blocks * shard_rows, observations)
    mine = lax.broadcasted_iota(jnp.int32, shape, 0)
    mine = mine // shard_rows * (shard_rows * col_count) + lax.rem(mine, shard_rows)
    mine = mine + col * shard_rows == lax.broadcasted_iota(jnp.int32, shape, 1)
    weight = lax.dot_general(
        jnp.where(mine, 1.0, 0.0), jnp.broadcast_to(weights, (lanes, observations)),
        (((1,), (1,)), ((), ())),
        precision=lax.Precision.HIGHEST, preferred_element_type=jnp.float32,
    )
    for place in range(col_count):
        near_left = place if place < half else col_count - 1 - (place - half)
        near_right = col_count - 1 - near_left
        tile = start + jnp.where(is_right, near_right, near_left)
        position = jnp.sum(jnp.where(tiles == tile, spot, 0))
        column = design_tile(tile, position // row_count, legendre, table)
        column = weight * column.astype(jnp.float32)
        column = jnp.where(lax.rem(position, row_count) == row, column, 0.0)
        output[place] = column.astype(jnp.bfloat16)


def design_kernel(offset, listed, legendre, table, output):
    def step(index, carry):
        output[index] = design_tile(
            listed[1, offset + index], listed[0, offset + index], legendre, table
        )
        return carry

    lax.fori_loop(0, output.shape[0], step, 0)


def factor_kernel(inner, half, *refs):
    streams, output = refs[:-1], refs[-1]
    rows, lanes = streams[0].shape[1:]
    col = lax.axis_index("col")
    spot = jnp.where(col >= half, 2 * half - 1 - col, col)
    for index, stream in enumerate(streams):
        here = pl.ds(index * rows, rows)
        kept = (spot > 0) | (index == 0)
        output[here, :lanes] = jnp.where(kept, stream[spot], jnp.zeros_like(stream[0]))
        if 1 <= index <= inner:
            output[here, lanes:] = jnp.zeros_like(stream[0])
        else:
            output[here, lanes:] = stream[0]


def stacked(streams, first, width):
    return jnp.concatenate(
        [jnp.concatenate([s[first + k] for s in streams], 0) for k in range(width)], 1
    )


def product_kernel(count, factor, *refs):
    streams, following, (own, *ends) = refs[:count], refs[count:-3], refs[-3:]
    lanes = own.shape[1]
    size = own.shape[0]
    col = lax.axis_index("col")
    is_end = (col == 0) | (col == lax.axis_size("col") - 1)

    def piece(first, width):
        both = lax.dot_general(
            stacked(streams, first, width), factor[...],
            (((0,), (0,)), ((), ())), preferred_element_type=jnp.float32,
        )
        for k in range(width):
            own[first + k] = both[k * lanes : (k + 1) * lanes, :lanes]
            end = both[k * lanes : (k + 1) * lanes, lanes:]
            high = end.astype(jnp.bfloat16)
            ends[0][first + k] = high
            ends[1][first + k] = (end - high.astype(jnp.float32)).astype(jnp.bfloat16)

    def step(index, carry):
        piece(2 * index, 2)
        return carry

    lax.fori_loop(0, size // 2, step, 0)
    if size % 2:
        piece(size - 1, 1)
    for later in following:
        @pl.when(is_end)
        def _(later=later):
            ends[0][: later.shape[0]] = later[...]
            ends[1][: later.shape[0]] = later[...]


def copy_kernel(offset, listed, resident, output, held, ins, outs):
    size = held.shape[0]

    def fetch(index):
        slot = listed[0, offset + index]
        return pltpu.make_async_copy(resident.at[slot], held.at[index], ins.at[index])

    def store(index):
        slot = listed[0, offset + index]
        return pltpu.make_async_copy(held.at[index], output.at[slot], outs.at[index])

    @pl.loop(0, size)
    def _(index):
        fetch(index).start()

    @pl.loop(0, size)
    def _(index):
        fetch(index).wait()
        store(index).start()

    @pl.loop(0, size)
    def _(index):
        store(index).wait()


def update_kernel(
    offset, listed, slab_start, own, high, low, resident, *refs,
):
    output, own_held, high_held, low_held, old, new, ins, outs, more = refs[-9:]
    size = old.shape[0]
    lanes = old.shape[1]
    col = lax.axis_index("col")
    column = slab_start[0] + col
    is_end = (col == 0) | (col == lax.axis_size("col") - 1)
    copies = [
        pltpu.make_async_copy(own, own_held, more.at[0]),
        pltpu.make_async_copy(high.at[pl.ds(0, size)], high_held, more.at[1]),
        pltpu.make_async_copy(low.at[pl.ds(0, size)], low_held, more.at[2]),
    ]

    def fetch(index):
        return pltpu.make_async_copy(
            resident.at[listed[0, offset + index]], old.at[index], ins.at[index]
        )

    def store(index):
        return pltpu.make_async_copy(
            new.at[index], output.at[listed[0, offset + index]], outs.at[index]
        )

    for copy in copies:
        copy.start()

    @pl.loop(0, size)
    def _(index):
        fetch(index).start()

    for copy in copies:
        copy.wait()

    @pl.loop(0, size)
    def _(index):
        fetch(index).wait()
        tile = listed[1, offset + index]
        keep = (tile >= column) & (tile * lanes < UNK)
        extra = high_held[index].astype(jnp.float32) + low_held[index].astype(jnp.float32)
        change = own_held[index] + jnp.where(is_end, extra, 0.0)
        new[index] = old[index] + jnp.where(keep, change, 0.0)
        store(index).start()

    @pl.loop(0, size)
    def _(index):
        store(index).wait()


def per_device(
    legendre, longitude, obs_weight, span_weight, span_of, tile_order, slab_start, resident
):
    block_count, shard_rows, slot_count, _, lanes = legendre.shape
    row_count = lax.axis_size("row")
    col_count = lax.axis_size("col")
    col_index = lax.axis_index("col")
    half = col_count // 2
    block_rows = shard_rows * col_count
    own_rows = block_count * shard_rows
    inner = half - 1
    bf16 = jnp.bfloat16
    smem, vmem, anywhere = whole(pltpu.SMEM), whole(), whole(pl.ANY)

    def mirrored(pairs):
        other = [(col_count - 1 - a, col_count - 1 - b) for a, b in pairs]
        return pairs + other

    inward = mirrored([(i, i + 1) for i in range(half - 1)])
    middles = [mirrored([(half - 1 - t, half)]) for t in range(half)]
    outward = mirrored([(i, i - 1) for i in range(2, half)])
    last_hop = mirrored([(1, 0)])
    filler = last_hop if half == 2 else []

    def shift(value, pairs, axis="col"):
        return lax.ppermute(value, axis, pairs)

    def streams_of(whole_item, near, far, idle=False):
        more = filler if idle else []
        ins = []
        for _ in range(inner):
            ins.append(shift(ins[-1] if ins else whole_item, inward + more))
        mids = [shift(far(whole_item), pairs + more * (t > 0)) for t, pairs in enumerate(middles)]
        froms = []
        for t in range(col_count - 2):
            piece = mids[t] if t < half else None
            if outward:
                moved = near(whole_item) if t == 0 else froms[-1]
                moved = shift(moved, outward)
                piece = moved if piece is None else piece + moved
            froms.append(piece)
        return [whole_item] + ins, froms

    def same(item):
        return item

    def own_part(values):
        values = values.reshape(block_count, block_rows)
        return lax.dynamic_slice_in_dim(values, col_index * shard_rows, shard_rows, 1)

    pages = PERIOD // lanes + 2
    lane_orders = jnp.arange(pages * lanes, dtype=jnp.int32) % PERIOD
    lane_orders = lane_orders.astype(jnp.float32).reshape(pages, 1, lanes)
    table = jnp.cos(own_part(longitude).reshape(1, own_rows, 1) * lane_orders)

    values = legendre.transpose(0, 2, 3, 1, 4).reshape(block_count, slot_count, shard_rows, lanes)
    old = resident.reshape(slot_count, lanes, lanes)
    counts = totals_of(slot_count)
    tile_shape = (own_rows, lanes)

    def tiles_of(size):
        return jax.ShapeDtypeStruct((size,) + tile_shape, bf16)

    def held(size):
        return pltpu.VMEM((size, lanes, lanes), jnp.float32)

    def sems(size):
        return pltpu.SemaphoreType.DMA((size,))

    def design(offset, size, listed, values, table):
        return pl.pallas_call(
            functools.partial(design_kernel, offset),
            out_shape=tiles_of(size),
            in_specs=[smem] + [vmem] * 2,
            out_specs=vmem,
            name="design",
        )(listed, values, table)

    listed, info, both = pl.pallas_call(
        functools.partial(plan_kernel, counts, row_count),
        out_shape=[
            jax.ShapeDtypeStruct((8, -(-slot_count // 128) * 128), jnp.int32),
            jax.ShapeDtypeStruct((1, 128), jnp.int32),
            tiles_of(col_count),
        ],
        in_specs=[smem] * 2 + [vmem] * 5,
        out_specs=[vmem] * 3,
        name="plan",
    )(slab_start, span_weight, tile_order, obs_weight, span_of, values, table)

    def collect(factors):
        return pl.pallas_call(
            functools.partial(factor_kernel, inner, half),
            out_shape=jax.ShapeDtypeStruct((len(factors) * own_rows, 2 * lanes), bf16),
            in_specs=[vmem] * len(factors),
            out_specs=vmem,
            name="factor",
        )(*factors)

    def copy_rest(offset, listed, old):
        size = slot_count - offset
        if not size:
            return []
        output = pl.pallas_call(
            functools.partial(copy_kernel, offset),
            in_specs=[smem, anywhere],
            out_specs=anywhere,
            out_shape=jax.ShapeDtypeStruct(old.shape, old.dtype),
            scratch_shapes=[held(size), sems(size), sems(size)],
        )(listed, old)
        return [output]

    def multiply(factor, streams, size, following):
        width = max([size] + [item.shape[0] for item in following])
        return pl.pallas_call(
            functools.partial(product_kernel, len(streams)),
            out_shape=[
                jax.ShapeDtypeStruct((size, lanes, lanes), jnp.float32),
                jax.ShapeDtypeStruct((width, lanes, lanes), bf16),
                jax.ShapeDtypeStruct((width, lanes, lanes), bf16),
            ],
            in_specs=[vmem] * (1 + len(streams) + len(following)),
            out_specs=[vmem] * 3,
            name="product",
        )(factor, *streams, *following)

    def update(offset, listed, slab_start, own, high, low, old, previous):
        size = own.shape[0]
        part = pltpu.VMEM((size, lanes, lanes), bf16)
        return pl.pallas_call(
            functools.partial(update_kernel, offset),
            in_specs=[smem] * 2 + [anywhere] * (4 + len(previous)),
            out_specs=anywhere,
            out_shape=jax.ShapeDtypeStruct(old.shape, old.dtype),
            scratch_shapes=[
                held(size), part, part, held(size), held(size),
                sems(size), sems(size), sems(3),
            ],
            input_output_aliases={6: 0} if previous else {},
            name="update",
        )(listed, slab_start, own, high, low, old, *previous)

    def branch(total):
        sizes = chunk_sizes(total)
        riding = half == 2 and own_rows == lanes

        def run(both, listed, slab_start, old, values, table):
            bit = 1
            while bit < row_count:
                pairs = [(r, r ^ bit) for r in range(row_count)]
                both = both + shift(both, pairs, "row")
                bit *= 2
            nears, froms = streams_of(both, lambda x: x[:half], lambda x: x[half:], True)
            factor = collect(nears + froms)
            offsets = [sum(sizes[:k]) for k in range(len(sizes))]
            designs = [
                design(offset, size, listed, values, table)
                for offset, size in zip(offsets, sizes)
            ]
            done = []
            for k, size in enumerate(sizes):
                if k < 2 or not riding:
                    nears, froms = streams_of(designs[k], same, same, k == 0)
                    streams = nears + froms
                else:
                    passed = shift(designs[k], middles[0])
                    near_end, far_end = done[k - 2][1:]
                    streams = [designs[k], near_end, passed, far_end]
                following = designs[k + 2 : k + 3] if riding else []
                own, high, low = multiply(factor, streams, size, following)
                more = [inward, middles[1]] if riding else [[], []]
                high = shift(high, last_hop + more[0])
                low = shift(low, last_hop + more[1])
                done.append((own, high, low))
            output = copy_rest(total, listed, old)
            for k, (own, high, low) in enumerate(done):
                output = [update(offsets[k], listed, slab_start, own, high, low, old, output)]
            return output[0]

        return run

    output = lax.switch(
        info[0, 0],
        [branch(total) for total in counts],
        both, listed, slab_start, old, values, table,
    )
    return output.reshape(resident.shape)


def solution(mesh):
    placed = (
        P(None, "col", None, "row", None),
        P(),
        P(),
        P(),
        P(),
        P(),
        P(),
        P(None, "row", "col", None, None),
    )
    return jax.shard_map(
        per_device,
        mesh=mesh,
        in_specs=placed,
        out_specs=P(None, "row", "col", None, None),
        check_vma=False,
    )
```

```python
import functools
import math

import jax
import jax.numpy as jnp
from jax import lax
from jax.experimental import pallas as pl
from jax.experimental.pallas import tpu as pltpu
from jax.sharding import PartitionSpec as P


DEGREE = 300
UNK = 90600
PERIOD = DEGREE + 1


def whole(space=pltpu.VMEM):
    return pl.BlockSpec(memory_space=space)


def totals_of(slot_count):
    counts = range(9, slot_count - 6, 16)
    return [count for count in counts if count < slot_count] + [slot_count]


def chunk_sizes(total):
    count = total // 15 + 2 if total > 12 else 1
    less = max(1, (total - 1 * (count // 2)) // count)
    sizes = [less + 1 * (k % 2) if count > 1 else total for k in range(count)]
    for k in (list(range(1, count, 2)) + list(range(0, count, 2)))[: total - sum(sizes)]:
        sizes[k] += 1
    return sizes


def design_tile(tile, slot, legendre, table):
    blocks, _, rows, lanes = legendre.shape
    start = lax.rem(tile * lanes, PERIOD)
    base = start // lanes
    shift = start - base * lanes
    turn = lax.rem(lanes - shift, lanes)
    lane = lax.broadcasted_iota(jnp.int32, (blocks * rows, lanes), 1)
    low = pltpu.roll(table[base], turn, 1)
    high = pltpu.roll(table[base + 1], turn, 1)
    wave = jnp.where(lane < lanes - shift, low, high)
    values = legendre[:, slot].astype(jnp.float32).reshape(blocks * rows, lanes)
    result = jnp.where(lane < UNK - tile * lanes, values * wave, 0.0)
    return result.astype(jnp.bfloat16)


def plan_kernel(
    counts, row_count, slab_start, span_weight, order, obs_weight, span_of, legendre, table,
    listed, info, output,
):
    lanes = legendre.shape[3]
    total = order.shape[0]
    width = listed.shape[1]
    start = slab_start[0]
    row = lax.axis_index("row")
    col = lax.axis_index("col")
    tiles = order[...].reshape(1, total)
    spot = lax.broadcasted_iota(jnp.int32, (1, total), 1)
    needed = (tiles >= start) & (tiles * lanes < UNK)
    rows = lax.broadcasted_iota(jnp.int32, (row_count, total), 0)
    matches = jnp.broadcast_to(jnp.where(needed, 1, 0), rows.shape)
    matches = jnp.where(lax.rem(spot, row_count) == rows, matches, 0)
    most = jnp.max(jnp.sum(matches, axis=1))
    choice = jnp.int32(0)
    for below in counts[:-1]:
        choice += jnp.where(most > below, 1, 0)

    mine = lax.rem(spot, row_count) == row
    own = jnp.where(needed & mine, 1.0, 0.0)
    before = jnp.dot(
        jnp.broadcast_to(own, (8, total)).astype(jnp.bfloat16),
        (
            lax.broadcasted_iota(jnp.int32, (total, total), 0)
            < lax.broadcasted_iota(jnp.int32, (total, total), 1)
        ).astype(jnp.float32).astype(jnp.bfloat16),
        preferred_element_type=jnp.float32,
    )[:1]
    slot = (spot // row_count).astype(jnp.float32)
    target = jnp.where(needed, before, jnp.sum(own) + slot - before)
    target = jnp.where(mine, target, -1.0)
    ids = lax.broadcasted_iota(jnp.int32, (width, total), 0).astype(jnp.float32)
    hits = jnp.where(ids == target, 1.0, 0.0)
    pair = lax.broadcasted_iota(jnp.int32, (8, total), 0)
    pair = jnp.where(pair == 0, slot, tiles.astype(jnp.float32))
    found = lax.dot_general(
        pair, hits, (((1,), (1,)), ((), ())),
        precision=lax.Precision.HIGHEST, preferred_element_type=jnp.float32,
    )
    listed[...] = found.astype(jnp.int32)
    info[...] = jnp.broadcast_to(choice, info.shape)

    col_count = output.shape[0]
    half = col_count // 2
    is_right = col >= half
    observations = obs_weight.shape[0]
    blocks, _, shard_rows, _ = legendre.shape
    span = span_of[...].reshape(1, observations)
    factor = jnp.zeros(span.shape, jnp.float32)
    for group in range(span_weight.shape[0]):
        factor += jnp.where(span == group, span_weight[group], 0.0)
    weights = obs_weight[...].reshape(1, observations) * factor
    weights *= 0.25 / math.sqrt(observations)
    shape = (blocks * shard_rows, observations)
    mine = lax.broadcasted_iota(jnp.int32, shape, 0)
    mine = mine // shard_rows * (shard_rows * col_count) + lax.rem(mine, shard_rows)
    mine = mine + col * shard_rows == lax.broadcasted_iota(jnp.int32, shape, 1)
    weight = lax.dot_general(
        jnp.where(mine, 1.0, 0.0), jnp.broadcast_to(weights, (lanes, observations)),
        (((1,), (1,)), ((), ())),
        precision=lax.Precision.HIGHEST, preferred_element_type=jnp.float32,
    )
    for place in range(col_count):
        near_left = place if place < half else col_count - 1 - (place - half)
        near_right = col_count - 1 - near_left
        tile = start + jnp.where(is_right, near_right, near_left)
        position = jnp.sum(jnp.where(tiles == tile, spot, 0))
        column = design_tile(tile, position // row_count, legendre, table)
        column = weight * column.astype(jnp.float32)
        column = jnp.where(lax.rem(position, row_count) == row, column, 0.0)
        output[place] = column.astype(jnp.bfloat16)


def design_kernel(offset, listed, legendre, table, *outputs):
    for output in outputs:
        def step(index, carry, output=output, offset=offset):
            output[index] = design_tile(
                listed[1, offset + index], listed[0, offset + index], legendre, table
            )
            return carry

        lax.fori_loop(0, output.shape[0], step, 0)
        offset += output.shape[0]


def factor_kernel(inner, half, *refs):
    streams, output = refs[:-1], refs[-1]
    rows, lanes = streams[0].shape[1:]
    col = lax.axis_index("col")
    spot = jnp.where(col >= half, 2 * half - 1 - col, col)
    for index, stream in enumerate(streams):
        here = pl.ds(index * rows, rows)
        kept = (spot > 0) | (index == 0)
        output[here, :lanes] = jnp.where(kept, stream[spot], jnp.zeros_like(stream[0]))
        if 1 <= index <= inner:
            output[here, lanes:] = jnp.zeros_like(stream[0])
        else:
            output[here, lanes:] = stream[0]


def stacked(streams, first, width):
    return jnp.concatenate(
        [jnp.concatenate([s[first + k] for s in streams], 0) for k in range(width)], 1
    )


def product_kernel(count, factor, *refs):
    streams, following, (own, *ends) = refs[:count], refs[count:-3], refs[-3:]
    lanes = own.shape[1]
    size = own.shape[0]
    col = lax.axis_index("col")
    is_end = (col == 0) | (col == lax.axis_size("col") - 1)

    def piece(first, width):
        both = lax.dot_general(
            stacked(streams, first, width), factor[...],
            (((0,), (0,)), ((), ())), preferred_element_type=jnp.float32,
        )
        for k in range(width):
            own[first + k] = both[k * lanes : (k + 1) * lanes, :lanes]
            end = both[k * lanes : (k + 1) * lanes, lanes:]
            high = end.astype(jnp.bfloat16)
            ends[0][first + k] = high
            ends[1][first + k] = (end - high.astype(jnp.float32)).astype(jnp.bfloat16)

    def step(index, carry):
        piece(2 * index, 2)
        return carry

    lax.fori_loop(0, size // 2, step, 0)
    if size % 2:
        piece(size - 1, 1)
    for later in following:
        @pl.when(is_end)
        def _(later=later):
            ends[0][: later.shape[0]] = later[...]
            ends[1][: later.shape[0]] = later[...]


def copy_kernel(offset, listed, resident, output, held, ins, outs):
    size = held.shape[0]

    def fetch(index):
        slot = listed[0, offset + index]
        return pltpu.make_async_copy(resident.at[slot], held.at[index], ins.at[index])

    def store(index):
        slot = listed[0, offset + index]
        return pltpu.make_async_copy(held.at[index], output.at[slot], outs.at[index])

    @pl.loop(0, size)
    def _(index):
        fetch(index).start()

    @pl.loop(0, size)
    def _(index):
        fetch(index).wait()
        store(index).start()

    @pl.loop(0, size)
    def _(index):
        store(index).wait()


def update_kernel(
    offset, listed, slab_start, own, high, low, resident, *refs,
):
    output, own_held, high_held, low_held, old, new, ins, outs, more = refs[-9:]
    size = old.shape[0]
    lanes = old.shape[1]
    col = lax.axis_index("col")
    column = slab_start[0] + col
    is_end = (col == 0) | (col == lax.axis_size("col") - 1)
    copies = [
        pltpu.make_async_copy(own, own_held, more.at[0]),
        pltpu.make_async_copy(high.at[pl.ds(0, size)], high_held, more.at[1]),
        pltpu.make_async_copy(low.at[pl.ds(0, size)], low_held, more.at[2]),
    ]

    def fetch(index):
        return pltpu.make_async_copy(
            resident.at[listed[0, offset + index]], old.at[index], ins.at[index]
        )

    def store(index):
        return pltpu.make_async_copy(
            new.at[index], output.at[listed[0, offset + index]], outs.at[index]
        )

    for copy in copies:
        copy.start()

    @pl.loop(0, size)
    def _(index):
        fetch(index).start()

    for copy in copies:
        copy.wait()

    @pl.loop(0, size)
    def _(index):
        fetch(index).wait()
        tile = listed[1, offset + index]
        keep = (tile >= column) & (tile * lanes < UNK)
        extra = high_held[index].astype(jnp.float32) + low_held[index].astype(jnp.float32)
        change = own_held[index] + jnp.where(is_end, extra, 0.0)
        new[index] = old[index] + jnp.where(keep, change, 0.0)
        store(index).start()

    @pl.loop(0, size)
    def _(index):
        store(index).wait()


def per_device(
    legendre, longitude, obs_weight, span_weight, span_of, tile_order, slab_start, resident
):
    block_count, shard_rows, slot_count, _, lanes = legendre.shape
    row_count = lax.axis_size("row")
    col_count = lax.axis_size("col")
    col_index = lax.axis_index("col")
    half = col_count // 2
    block_rows = shard_rows * col_count
    own_rows = block_count * shard_rows
    inner = half - 1
    bf16 = jnp.bfloat16
    smem, vmem, anywhere = whole(pltpu.SMEM), whole(), whole(pl.ANY)

    def mirrored(pairs):
        other = [(col_count - 1 - a, col_count - 1 - b) for a, b in pairs]
        return pairs + other

    inward = mirrored([(i, i + 1) for i in range(half - 1)])
    middles = [mirrored([(half - 1 - t, half)]) for t in range(half)]
    outward = mirrored([(i, i - 1) for i in range(2, half)])
    last_hop = mirrored([(1, 0)])
    filler = last_hop if half == 2 else []

    def shift(value, pairs, axis="col"):
        return lax.ppermute(value, axis, pairs)

    def streams_of(whole_item, near, far, idle=False):
        more = filler if idle else []
        ins = []
        for _ in range(inner):
            ins.append(shift(ins[-1] if ins else whole_item, inward + more))
        mids = [shift(far(whole_item), pairs + more * (t > 0)) for t, pairs in enumerate(middles)]
        froms = []
        for t in range(col_count - 2):
            piece = mids[t] if t < half else None
            if outward:
                moved = near(whole_item) if t == 0 else froms[-1]
                moved = shift(moved, outward)
                piece = moved if piece is None else piece + moved
            froms.append(piece)
        return [whole_item] + ins, froms

    def same(item):
        return item

    def own_part(values):
        values = values.reshape(block_count, block_rows)
        return lax.dynamic_slice_in_dim(values, col_index * shard_rows, shard_rows, 1)

    pages = PERIOD // lanes + 2
    lane_orders = jnp.arange(pages * lanes, dtype=jnp.int32) % PERIOD
    lane_orders = lane_orders.astype(jnp.float32).reshape(pages, 1, lanes)
    table = jnp.cos(own_part(longitude).reshape(1, own_rows, 1) * lane_orders)

    values = legendre.transpose(0, 2, 3, 1, 4).reshape(block_count, slot_count, shard_rows, lanes)
    old = resident.reshape(slot_count, lanes, lanes)
    counts = totals_of(slot_count)
    tile_shape = (own_rows, lanes)

    def tiles_of(size):
        return jax.ShapeDtypeStruct((size,) + tile_shape, bf16)

    def held(size):
        return pltpu.VMEM((size, lanes, lanes), jnp.float32)

    def sems(size):
        return pltpu.SemaphoreType.DMA((size,))

    def design(offset, parts, listed, values, table):
        return pl.pallas_call(
            functools.partial(design_kernel, offset),
            out_shape=[tiles_of(size) for size in parts],
            in_specs=[smem] + [vmem] * 2,
            out_specs=[vmem] * len(parts),
            name="design",
        )(listed, values, table)

    listed, info, both = pl.pallas_call(
        functools.partial(plan_kernel, counts, row_count),
        out_shape=[
            jax.ShapeDtypeStruct((8, -(-slot_count // 128) * 128), jnp.int32),
            jax.ShapeDtypeStruct((1, 128), jnp.int32),
            tiles_of(col_count),
        ],
        in_specs=[smem] * 2 + [vmem] * 5,
        out_specs=[vmem] * 3,
        name="plan",
    )(slab_start, span_weight, tile_order, obs_weight, span_of, values, table)

    def collect(factors):
        return pl.pallas_call(
            functools.partial(factor_kernel, inner, half),
            out_shape=jax.ShapeDtypeStruct((len(factors) * own_rows, 2 * lanes), bf16),
            in_specs=[vmem] * len(factors),
            out_specs=vmem,
            name="factor",
        )(*factors)

    def copy_rest(offset, listed, old):
        size = slot_count - offset
        if not size:
            return []
        output = pl.pallas_call(
            functools.partial(copy_kernel, offset),
            in_specs=[smem, anywhere],
            out_specs=anywhere,
            out_shape=jax.ShapeDtypeStruct(old.shape, old.dtype),
            scratch_shapes=[held(size), sems(size), sems(size)],
        )(listed, old)
        return [output]

    def multiply(factor, streams, size, following):
        width = max([size] + [item.shape[0] for item in following])
        return pl.pallas_call(
            functools.partial(product_kernel, len(streams)),
            out_shape=[
                jax.ShapeDtypeStruct((size, lanes, lanes), jnp.float32),
                jax.ShapeDtypeStruct((width, lanes, lanes), bf16),
                jax.ShapeDtypeStruct((width, lanes, lanes), bf16),
            ],
            in_specs=[vmem] * (1 + len(streams) + len(following)),
            out_specs=[vmem] * 3,
            name="product",
        )(factor, *streams, *following)

    def update(offset, listed, slab_start, own, high, low, old, previous):
        size = own.shape[0]
        part = pltpu.VMEM((size, lanes, lanes), bf16)
        return pl.pallas_call(
            functools.partial(update_kernel, offset),
            in_specs=[smem] * 2 + [anywhere] * (4 + len(previous)),
            out_specs=anywhere,
            out_shape=jax.ShapeDtypeStruct(old.shape, old.dtype),
            scratch_shapes=[
                held(size), part, part, held(size), held(size),
                sems(size), sems(size), sems(3),
            ],
            input_output_aliases={6: 0} if previous else {},
            name="update",
        )(listed, slab_start, own, high, low, old, *previous)

    def branch(total):
        sizes = chunk_sizes(total)
        riding = half == 2 and own_rows == lanes

        def run(both, listed, slab_start, old, values, table):
            bit = 1
            while bit < row_count:
                pairs = [(r, r ^ bit) for r in range(row_count)]
                both = both + shift(both, pairs, "row")
                bit *= 2
            nears, froms = streams_of(both, lambda x: x[:half], lambda x: x[half:], True)
            factor = collect(nears + froms)
            offsets = [sum(sizes[:k]) for k in range(len(sizes))]
            designs = []
            while len(designs) < len(sizes):
                k = len(designs)
                parts = sizes[k : k + (2 if k == 1 else 1)]
                designs += design(offsets[k], parts, listed, values, table)
            done = []
            for k, size in enumerate(sizes):
                if k < 2 or not riding:
                    nears, froms = streams_of(designs[k], same, same, k == 0)
                    streams = nears + froms
                else:
                    passed = shift(designs[k], middles[0])
                    near_end, far_end = done[k - 2][1:]
                    streams = [designs[k], near_end, passed, far_end]
                following = designs[k + 2 : k + 3] if riding else []
                own, high, low = multiply(factor, streams, size, following)
                more = [inward, middles[1]] if riding else [[], []]
                high = shift(high, last_hop + more[0])
                low = shift(low, last_hop + more[1])
                done.append((own, high, low))
            output = copy_rest(total, listed, old)
            for k, (own, high, low) in enumerate(done):
                output = [update(offsets[k], listed, slab_start, own, high, low, old, output)]
            return output[0]

        return run

    output = lax.switch(
        info[0, 0],
        [branch(total) for total in counts],
        both, listed, slab_start, old, values, table,
    )
    return output.reshape(resident.shape)


def solution(mesh):
    placed = (
        P(None, "col", None, "row", None),
        P(),
        P(),
        P(),
        P(),
        P(),
        P(),
        P(None, "row", "col", None, None),
    )
    return jax.shard_map(
        per_device,
        mesh=mesh,
        in_specs=placed,
        out_specs=P(None, "row", "col", None, None),
        check_vma=False,
    )
```
